32 devices in a mesh: slab: 4 (over x, core), row: 8 (over z, y).
Axes of the slice: x: 2, y: 2, z: 4, core: 2. Of those that a mesh axis runs over, the one named last changes fastest.
Arguments:
- rhs: bfloat16 [3, 2, 64, 8192], P(None, None, None, 'row'), may hold values from -6 to 6
- operator: bfloat16 [4, 2, 8192, 8192], P('slab', None, 'row'), may hold values from -0.046875 to 0.046875
- sources: bfloat16 [4, 3, 2, 64, 8192], P('slab', None, None, None, 'row'), may hold values from -6 to 6
- skeleton: int32 [4, 8192], P('slab'), may hold values from 0 to 8191, each once within a row
Outputs:
- outgoing: bfloat16 [4, 3, 2, 64, 8192], P('slab', None, None, None, 'row')
The draws below stay inside these ranges and needn't reach their ends.
Inputs may be any that keep to these rules, and one draw needn't show every extreme that they name: Each row of skeleton is a permutation of 0 to 8191.
All inputs are finite; a program needn't handle non-finite values.
Results may differ from the reference program's by a relative error of at most 0.0055.
Values may be sent and summed in bfloat16 or wider, within the bound.
A program may use at most 192 MiB of HBM per device.

```python
import jax
import jax.numpy as jnp
from jax import lax

NI = 8192
B = 64
NB = 3
S = 4
N_SLAB = 4


def block_scale(key, shape, cuts, smallest, high):
    level, own = 1.0, jax.random.fold_in(key, 6)
    for axis_at, parts in cuts:
        heights = jnp.exp(jax.random.uniform(jax.random.fold_in(own, axis_at), (parts,), jnp.float32, smallest / len(cuts), high / len(cuts)))
        level = level * jnp.repeat(heights, shape[axis_at] // parts).reshape([-1 if axis == axis_at else 1 for axis in range(len(shape))])
    return level


def centred(stream_key, shape, scale, limit, shards=(), kind=jnp.bfloat16):
    gain = block_scale(stream_key, shape, shards, -0.22, 0.18) if shards else 1.0
    array = jax.random.normal(stream_key, shape, jnp.float32) * scale * gain
    return jnp.minimum(jnp.maximum(array, -limit), limit).astype(kind)


def setup_inputs(seed: int = 0) -> dict:
    seeds = jax.random.split(jax.random.key(seed), 5)
    rhs = centred(seeds[0], (NB, 2, B, NI), 1.0, 6.0, ((3, 8),))
    operator = centred(seeds[1], (S, 2, NI, NI), (2 * NI) ** -0.5, 0.046875, ((0, 4), (2, 8)))
    sources = centred(seeds[2], (S, NB, 2, B, NI), 1.0, 6.0, ((0, 4), (4, 8)))
    skeleton = jax.vmap(lambda own: jax.random.permutation(own, NI))(jax.random.split(seeds[3], S)).reshape((S, NI)).astype(jnp.int32)
    return {"rhs": rhs, "operator": operator, "sources": sources, "skeleton": skeleton}


def complex_apply(inputs, matrix):
    count = inputs.shape[0]
    width = inputs.shape[2]
    depth = inputs.shape[3]
    rows = matrix.shape[1]
    flat = inputs.reshape(count * 2 * width, depth)
    mflat = matrix.reshape(2 * rows, depth)
    joined = lax.dot_general(flat, mflat, (((1,), (1,)), ((), ())), preferred_element_type=jnp.float32)
    joined = joined.reshape(count, 2, width, 2, rows)
    real_part = joined[:, 0, :, 0] - joined[:, 1, :, 1]
    imag_part = joined[:, 1, :, 0] + joined[:, 0, :, 1]
    return jnp.stack([real_part, imag_part], axis=1)


def reference(rhs, operator, sources, skeleton):
    incoming = rhs
    results = []
    for section in range(N_SLAB):
        ordered = jnp.take(incoming, skeleton[section].astype(jnp.int32), axis=3)
        value = complex_apply(ordered, operator[section]) + sources[section].astype(jnp.float32)
        value = value.astype(jnp.bfloat16)
        results.append(value)
        incoming = value
    return jnp.stack(results)
```

```python
import functools

import jax
import jax.numpy as jnp
from jax import lax
from jax.experimental import pallas as pl
from jax.experimental.pallas import tpu as pltpu
from jax.sharding import PartitionSpec as P

MESH = pl.DeviceIdType.MESH


def ring_to_row(position, count):
    return jnp.where(position < count // 2, 2 * position, 2 * (count - 1 - position) + 1)


def row_to_ring(row, count):
    return jnp.where(row % 2 == 0, row // 2, count - 1 - row // 2)


def kernel(
    slabs, count,
    skel, rhs, op, src, out,
    matrix, recv, xf, xg, xb, acc,
    msem, lsem, right_send, right_recv, left_send, left_recv, pass_send, pass_recv,
):
    batches = rhs.shape[0]
    rows = rhs.shape[1]
    width = rhs.shape[2]
    depth = rows * count
    half = width // 2
    slab = lax.axis_index("slab")
    row = lax.axis_index("row")
    place = row_to_ring(row, count)
    right = ring_to_row((place + 1) % count, count)
    left = ring_to_row((place + count - 1) % count, count)
    first = slab == 0
    inner = slab < slabs - 1

    loads = [
        pltpu.make_async_copy(op.at[pl.ds(part * rows, rows)], matrix.at[pl.ds(part * rows, rows)], msem.at[part])
        for part in range(2)
    ]

    barrier = pltpu.get_barrier_semaphore()
    pl.semaphore_signal(barrier, inc=1, device_id={"slab": slab, "row": right}, device_id_type=MESH)
    pl.semaphore_signal(barrier, inc=1, device_id={"slab": slab, "row": left}, device_id_type=MESH)

    @pl.when(inner)
    def _():
        pl.semaphore_signal(barrier, inc=1, device_id={"slab": slab + 1, "row": row}, device_id_type=MESH)

    @pl.when(jnp.logical_not(first))
    def _():
        pl.semaphore_signal(barrier, inc=1, device_id={"slab": slab - 1, "row": row}, device_id_type=MESH)

    for copy in loads:
        copy.start()
    pl.semaphore_wait(barrier, 2 + jnp.where(inner, 1, 0) + jnp.where(first, 0, 1))

    def block(owner):
        return pl.ds(pl.multiple_of(owner * rows, rows), rows)

    def rightward(batch, step):
        owner = ring_to_row((place + count - step) % count, count)
        piece = recv.at[batch, block(owner)]
        return pltpu.make_async_remote_copy(
            src_ref=piece, dst_ref=piece,
            send_sem=right_send.at[batch, step], recv_sem=right_recv.at[batch, step],
            device_id={"slab": slab, "row": right}, device_id_type=MESH,
        )

    def leftward(batch, step):
        owner = ring_to_row((place + step) % count, count)
        piece = recv.at[batch, block(owner)]
        return pltpu.make_async_remote_copy(
            src_ref=piece, dst_ref=piece,
            send_sem=left_send.at[batch, step], recv_sem=left_recv.at[batch, step],
            device_id={"slab": slab, "row": left}, device_id_type=MESH,
        )

    right_steps = count // 2
    left_steps = count - 1 - right_steps

    def passing(batch):
        return pltpu.make_async_remote_copy(
            src_ref=out.at[batch], dst_ref=recv.at[batch, block(row)],
            send_sem=pass_send.at[batch], recv_sem=pass_recv.at[batch],
            device_id={"slab": jnp.minimum(slab + 1, slabs - 1), "row": row}, device_id_type=MESH,
        )

    def own(batch):
        return pltpu.make_async_copy(rhs.at[batch], recv.at[batch, block(row)], lsem.at[batch])

    def advance(batch, step):
        if step == 0:
            @pl.when(first)
            def _():
                own(batch).start()
                own(batch).wait()

            @pl.when(jnp.logical_not(first))
            def _():
                passing(batch).wait_recv()
        else:
            if step - 1 < right_steps:
                rightward(batch, step - 1).wait_recv()
            if step - 1 < left_steps:
                leftward(batch, step - 1).wait_recv()
        if step < right_steps:
            rightward(batch, step).start()
        if step < left_steps:
            leftward(batch, step).start()

    steps = right_steps + 1
    parts = 8
    span = depth // parts
    unroll = 64
    done = 0

    for batch in range(batches):
        for step in range(done, steps):
            advance(batch, step)

        @pl.loop(0, parts)
        def _(part):
            at = pl.ds(pl.multiple_of(part * span, span), span)
            xf[at, :] = recv[batch, at, :].astype(jnp.float32)

        acc[...] = jnp.zeros_like(acc)
        if batch == 0:
            for copy in loads:
                copy.wait()

        def piece(part):
            base = part * span

            @pl.loop(0, span // unroll)
            def _(chunk):
                for inner_row in range(unroll):
                    index = chunk * unroll + inner_row
                    xg[pl.ds(index, 1), :] = xf[pl.ds(skel[base + index], 1), :]

            xb[...] = xg[...].astype(jnp.bfloat16)
            acc[...] += jnp.dot(
                matrix[:, pl.ds(pl.multiple_of(base, span), span)], xb[...],
                preferred_element_type=jnp.float32,
            )

        @pl.loop(0, parts)
        def _(part):
            piece(part)

        lane = lax.broadcasted_iota(jnp.int32, (rows, width), 1)
        turned = pltpu.roll(acc[rows:, :], half, axis=1)
        total = acc[:rows, :] + jnp.where(lane < half, -turned, turned)
        out[batch] = (total + src[batch].astype(jnp.float32)).astype(jnp.bfloat16)

        @pl.when(inner)
        def _():
            passing(batch).start()

    for batch in range(batches):
        for step in range(right_steps):
            rightward(batch, step).wait_send()
        for step in range(left_steps):
            leftward(batch, step).wait_send()

        @pl.when(inner)
        def _():
            passing(batch).wait_send()


def on_device(rhs, operator, sources, skeleton):
    slabs = lax.axis_size("slab")
    count = lax.axis_size("row")
    batches, two, lanes, rows = rhs.shape
    depth = operator.shape[3]
    width = two * lanes
    flipped = rhs.reshape(batches, width, rows).transpose(0, 2, 1)
    added = sources[0].reshape(batches, width, rows).transpose(0, 2, 1)
    half = max(1, count // 2)
    result = pl.pallas_call(
        functools.partial(kernel, slabs, count),
        out_shape=jax.ShapeDtypeStruct((batches, rows, width), jnp.bfloat16),
        in_specs=[
            pl.BlockSpec(memory_space=pltpu.SMEM),
            pl.BlockSpec(memory_space=pltpu.VMEM),
            pl.BlockSpec(memory_space=pl.ANY),
            pl.BlockSpec(memory_space=pltpu.VMEM),
        ],
        out_specs=pl.BlockSpec(memory_space=pltpu.VMEM),
        scratch_shapes=[
            pltpu.VMEM((2 * rows, depth), jnp.bfloat16),
            pltpu.VMEM((batches, depth, width), jnp.bfloat16),
            pltpu.VMEM((depth, width), jnp.float32),
            pltpu.VMEM((depth // 8, width), jnp.float32),
            pltpu.VMEM((depth // 8, width), jnp.bfloat16),
            pltpu.VMEM((2 * rows, width), jnp.float32),
            pltpu.SemaphoreType.DMA((2,)),
            pltpu.SemaphoreType.DMA((batches,)),
            pltpu.SemaphoreType.DMA((batches, half)),
            pltpu.SemaphoreType.DMA((batches, half)),
            pltpu.SemaphoreType.DMA((batches, half)),
            pltpu.SemaphoreType.DMA((batches, half)),
            pltpu.SemaphoreType.DMA((batches,)),
            pltpu.SemaphoreType.DMA((batches,)),
        ],
        compiler_params=pltpu.CompilerParams(
            collective_id=0, has_side_effects=True, vmem_limit_bytes=60 * 1024 * 1024
        ),
    )(skeleton[0], flipped, operator[0].reshape(2 * rows, depth), added)
    return result.transpose(0, 2, 1).reshape(batches, two, lanes, rows)[None]


def solution(mesh):
    return jax.shard_map(
        on_device,
        mesh=mesh,
        in_specs=(
            P(None, None, None, "row"),
            P("slab", None, "row", None),
            P("slab", None, None, None, "row"),
            P("slab", None),
        ),
        out_specs=P("slab", None, None, None, "row"),
        check_vma=False,
    )
```

```python
import functools

import jax
import jax.numpy as jnp
from jax import lax
from jax.experimental import pallas as pl
from jax.experimental.pallas import tpu as pltpu
from jax.sharding import PartitionSpec as P

MESH = pl.DeviceIdType.MESH


def ring_to_row(position, count):
    return jnp.where(position < count // 2, 2 * position, 2 * (count - 1 - position) + 1)


def row_to_ring(row, count):
    return jnp.where(row % 2 == 0, row // 2, count - 1 - row // 2)


MARKS = (1, 2, 4, 5, 6)


def kernel(
    slabs, count, pieces,
    skel, rhs, op, src, out,
    matrix, recv, xf, xb,
    msem, lsem, right_send, right_recv, left_send, left_recv, pass_send, pass_recv,
):
    batches = rhs.shape[0]
    rows = rhs.shape[1]
    width = rhs.shape[2]
    depth = rows * count
    half = width // 2
    size = rows // pieces
    slab = lax.axis_index("slab")
    row = lax.axis_index("row")
    place = row_to_ring(row, count)
    right = ring_to_row((place + 1) % count, count)
    left = ring_to_row((place + count - 1) % count, count)
    first = slab == 0
    inner = slab < slabs - 1
    right_steps = count // 2
    left_steps = count - 1 - right_steps

    def load(piece, part):
        return pltpu.make_async_copy(
            op.at[part, pl.ds(piece * size, size)],
            matrix.at[pl.ds((2 * piece + part) * size, size)],
            msem.at[piece, part],
        )

    barrier = pltpu.get_barrier_semaphore()
    pl.semaphore_signal(barrier, inc=1, device_id={"slab": slab, "row": right}, device_id_type=MESH)
    pl.semaphore_signal(barrier, inc=1, device_id={"slab": slab, "row": left}, device_id_type=MESH)

    @pl.when(inner)
    def _():
        pl.semaphore_signal(barrier, inc=1, device_id={"slab": slab + 1, "row": row}, device_id_type=MESH)

    @pl.when(jnp.logical_not(first))
    def _():
        pl.semaphore_signal(barrier, inc=1, device_id={"slab": slab - 1, "row": row}, device_id_type=MESH)

    def own(batch):
        return pltpu.make_async_copy(
            rhs.at[batch], recv.at[batch, pl.ds(pl.multiple_of(row * rows, rows), rows)], lsem.at[batch]
        )

    @pl.when(first)
    def _():
        for batch in range(batches):
            own(batch).start()

    for piece in range(pieces):
        for part in range(2):
            load(piece, part).start()

    @pl.when(first)
    def _():
        for batch in range(batches):
            own(batch).wait()

    pl.semaphore_wait(barrier, 2 + jnp.where(inner, 1, 0) + jnp.where(first, 0, 1))

    def held(batch, owner, piece):
        return recv.at[batch, pl.ds(pl.multiple_of(owner * rows + piece * size, size), size)]

    def rightward(batch, piece, step):
        data = held(batch, ring_to_row((place + count - step) % count, count), piece)
        return pltpu.make_async_remote_copy(
            src_ref=data, dst_ref=data,
            send_sem=right_send.at[batch, piece, step], recv_sem=right_recv.at[batch, piece, step],
            device_id={"slab": slab, "row": right}, device_id_type=MESH,
        )

    def leftward(batch, piece, step):
        data = held(batch, ring_to_row((place + step) % count, count), piece)
        return pltpu.make_async_remote_copy(
            src_ref=data, dst_ref=data,
            send_sem=left_send.at[batch, piece, step], recv_sem=left_recv.at[batch, piece, step],
            device_id={"slab": slab, "row": left}, device_id_type=MESH,
        )

    def passing(batch, piece):
        return pltpu.make_async_remote_copy(
            src_ref=out.at[batch, pl.ds(piece * size, size)], dst_ref=held(batch, row, piece),
            send_sem=pass_send.at[batch, piece], recv_sem=pass_recv.at[batch, piece],
            device_id={"slab": jnp.minimum(slab + 1, slabs - 1), "row": row}, device_id_type=MESH,
        )

    def splits(piece):
        if count % 2 or pieces == 1:
            return right_steps, left_steps
        if piece < pieces // 2:
            return count // 2, count // 2 - 1
        return count // 2 - 1, count // 2

    def advance(batch, piece, step):
        rights, lefts = splits(piece)
        if step == 0:
            @pl.when(jnp.logical_not(first))
            def _():
                passing(batch, piece).wait_recv()
        else:
            if step <= rights:
                rightward(batch, piece, step - 1).wait_recv()
            if step <= lefts:
                leftward(batch, piece, step - 1).wait_recv()
        if step < rights:
            rightward(batch, piece, step).start()
        if step < lefts:
            leftward(batch, piece, step).start()

    steps = right_steps + 1
    waves = steps + pieces - 1

    def wave(batch, now):
        for piece in range(pieces):
            if 0 <= now - piece < steps:
                advance(batch, piece, now - piece)

    def waves_of_next(batch, low, high):
        if low < high:
            @pl.when(batch + 1 < batches)
            def _():
                for now in range(low, high):
                    wave(batch + 1, now)

    for now in range(waves):
        wave(0, now)

    spread = 8
    group = 128
    marks = [min(waves, mark) for mark in MARKS]

    def gather(start, stop):
        @pl.loop(start, stop)
        def _(chunk):
            base = pl.multiple_of(chunk * group, group)
            for lump in range(group // 16):
                picked = [xf[pl.ds(skel[base + lump * 16 + offset], 1), :] for offset in range(16)]
                xb[pl.ds(pl.multiple_of(base + lump * 16, 16), 16), :] = jnp.concatenate(picked, axis=0).astype(jnp.bfloat16)

    @pl.loop(0, batches)
    def _(batch):
        span = depth // spread

        @pl.loop(0, spread)
        def _(part):
            at = pl.ds(pl.multiple_of(part * span, span), span)
            xf[at, :] = recv[batch, at, :].astype(jnp.float32)

        chunks = depth // group
        gather(0, chunks // 2)
        waves_of_next(batch, 0, marks[0])
        gather(chunks // 2, chunks)
        waves_of_next(batch, marks[0], marks[1])

        for piece in range(pieces):
            @pl.when(batch == 0)
            def _():
                for part in range(2):
                    load(piece, part).wait()

            joined = jnp.dot(
                matrix[pl.ds(2 * piece * size, 2 * size), :], xb[...], preferred_element_type=jnp.float32
            )
            lane = lax.broadcasted_iota(jnp.int32, (size, width), 1)
            turned = pltpu.roll(joined[size:], half, axis=1)
            total = joined[:size] + jnp.where(lane < half, -turned, turned)
            at = pl.ds(piece * size, size)
            out[batch, at, :] = (total + src[batch, at, :].astype(jnp.float32)).astype(jnp.bfloat16)

            @pl.when(inner)
            def _():
                passing(batch, piece).start()

            low = marks[min(len(marks) - 1, piece + 1)]
            high = waves if piece == pieces - 1 else marks[min(len(marks) - 1, piece + 2)]
            waves_of_next(batch, low, high)

    @pl.loop(0, batches)
    def _(batch):
        for piece in range(pieces):
            rights, lefts = splits(piece)
            for step in range(rights):
                rightward(batch, piece, step).wait_send()
            for step in range(lefts):
                leftward(batch, piece, step).wait_send()

            @pl.when(inner)
            def _():
                passing(batch, piece).wait_send()


def on_device(rhs, operator, sources, skeleton):
    slabs = lax.axis_size("slab")
    count = lax.axis_size("row")
    batches, two, lanes, rows = rhs.shape
    depth = operator.shape[3]
    width = two * lanes
    flipped = rhs.reshape(batches, width, rows).transpose(0, 2, 1)
    added = sources[0].reshape(batches, width, rows).transpose(0, 2, 1)
    half = max(1, count // 2)
    pieces = 4 if count <= 8 else 1
    result = pl.pallas_call(
        functools.partial(kernel, slabs, count, pieces),
        out_shape=jax.ShapeDtypeStruct((batches, rows, width), jnp.bfloat16),
        in_specs=[
            pl.BlockSpec(memory_space=pltpu.SMEM),
            pl.BlockSpec(memory_space=pltpu.VMEM),
            pl.BlockSpec(memory_space=pl.ANY),
            pl.BlockSpec(memory_space=pltpu.VMEM),
        ],
        out_specs=pl.BlockSpec(memory_space=pltpu.VMEM),
        scratch_shapes=[
            pltpu.VMEM((2 * rows, depth), jnp.bfloat16),
            pltpu.VMEM((batches, depth, width), jnp.bfloat16),
            pltpu.VMEM((depth, width), jnp.float32),
            pltpu.VMEM((depth, width), jnp.bfloat16),
            pltpu.SemaphoreType.DMA((pieces, 2)),
            pltpu.SemaphoreType.DMA((batches,)),
            pltpu.SemaphoreType.DMA((batches, pieces, half)),
            pltpu.SemaphoreType.DMA((batches, pieces, half)),
            pltpu.SemaphoreType.DMA((batches, pieces, half)),
            pltpu.SemaphoreType.DMA((batches, pieces, half)),
            pltpu.SemaphoreType.DMA((batches, pieces)),
            pltpu.SemaphoreType.DMA((batches, pieces)),
        ],
        compiler_params=pltpu.CompilerParams(
            collective_id=0, has_side_effects=True, vmem_limit_bytes=60 * 1024 * 1024
        ),
    )(skeleton[0], flipped, operator[0], added)
    return result.transpose(0, 2, 1).reshape(batches, two, lanes, rows)[None]


def solution(mesh):
    return jax.shard_map(
        on_device,
        mesh=mesh,
        in_specs=(
            P(None, None, None, "row"),
            P("slab", None, "row", None),
            P("slab", None, None, None, "row"),
            P("slab", None),
        ),
        out_specs=P("slab", None, None, None, "row"),
        check_vma=False,
    )
```

```python
import functools

import jax
import jax.numpy as jnp
from jax import lax
from jax.experimental import pallas as pl
from jax.experimental.pallas import tpu as pltpu
from jax.sharding import PartitionSpec as P

MESH = pl.DeviceIdType.MESH


def ring_to_row(position, count):
    return jnp.where(position < count // 2, 2 * position, 2 * (count - 1 - position) + 1)


def row_to_ring(row, count):
    return jnp.where(row % 2 == 0, row // 2, count - 1 - row // 2)


MARKS = (1, 2, 3, 4, 5, 6, 7)


def kernel(
    slabs, count, pieces,
    skel, rhs, op, src, out,
    matrix, recv, xf, xb,
    msem, lsem, right_send, right_recv, left_send, left_recv, pass_send, pass_recv,
):
    batches = rhs.shape[0]
    rows = rhs.shape[1]
    width = rhs.shape[2]
    depth = rows * count
    half = width // 2
    size = rows // pieces
    slab = lax.axis_index("slab")
    row = lax.axis_index("row")
    place = row_to_ring(row, count)
    right = ring_to_row((place + 1) % count, count)
    left = ring_to_row((place + count - 1) % count, count)
    first = slab == 0
    inner = slab < slabs - 1
    right_steps = count // 2
    left_steps = count - 1 - right_steps

    def load(piece, part):
        return pltpu.make_async_copy(
            op.at[part, pl.ds(piece * size, size)],
            matrix.at[pl.ds((2 * piece + part) * size, size)],
            msem.at[piece, part],
        )

    barrier = pltpu.get_barrier_semaphore()
    pl.semaphore_signal(barrier, inc=1, device_id={"slab": slab, "row": right}, device_id_type=MESH)
    pl.semaphore_signal(barrier, inc=1, device_id={"slab": slab, "row": left}, device_id_type=MESH)

    @pl.when(inner)
    def _():
        pl.semaphore_signal(barrier, inc=1, device_id={"slab": slab + 1, "row": row}, device_id_type=MESH)

    @pl.when(jnp.logical_not(first))
    def _():
        pl.semaphore_signal(barrier, inc=1, device_id={"slab": slab - 1, "row": row}, device_id_type=MESH)

    def own(batch):
        return pltpu.make_async_copy(
            rhs.at[batch], recv.at[batch, pl.ds(pl.multiple_of(row * rows, rows), rows)], lsem.at[batch]
        )

    @pl.when(first)
    def _():
        for batch in range(batches):
            own(batch).start()

    for piece in range(pieces):
        for part in range(2):
            load(piece, part).start()

    @pl.when(first)
    def _():
        for batch in range(batches):
            own(batch).wait()

    pl.semaphore_wait(barrier, 2 + jnp.where(inner, 1, 0) + jnp.where(first, 0, 1))

    def held(batch, owner, piece):
        return recv.at[batch, pl.ds(pl.multiple_of(owner * rows + piece * size, size), size)]

    def rightward(batch, piece, step):
        data = held(batch, ring_to_row((place + count - step) % count, count), piece)
        return pltpu.make_async_remote_copy(
            src_ref=data, dst_ref=data,
            send_sem=right_send.at[batch, piece, step], recv_sem=right_recv.at[batch, piece, step],
            device_id={"slab": slab, "row": right}, device_id_type=MESH,
        )

    def leftward(batch, piece, step):
        data = held(batch, ring_to_row((place + step) % count, count), piece)
        return pltpu.make_async_remote_copy(
            src_ref=data, dst_ref=data,
            send_sem=left_send.at[batch, piece, step], recv_sem=left_recv.at[batch, piece, step],
            device_id={"slab": slab, "row": left}, device_id_type=MESH,
        )

    def passing(batch, piece):
        return pltpu.make_async_remote_copy(
            src_ref=out.at[batch, pl.ds(piece * size, size)], dst_ref=held(batch, row, piece),
            send_sem=pass_send.at[batch, piece], recv_sem=pass_recv.at[batch, piece],
            device_id={"slab": jnp.minimum(slab + 1, slabs - 1), "row": row}, device_id_type=MESH,
        )

    def splits(piece):
        if count % 2 or pieces == 1:
            return right_steps, left_steps
        if piece < pieces // 2:
            return count // 2, count // 2 - 1
        return count // 2 - 1, count // 2

    def advance(batch, piece, step):
        rights, lefts = splits(piece)
        if step == 0:
            @pl.when(jnp.logical_not(first))
            def _():
                passing(batch, piece).wait_recv()
        else:
            if step <= rights:
                rightward(batch, piece, step - 1).wait_recv()
            if step <= lefts:
                leftward(batch, piece, step - 1).wait_recv()
        if step < rights:
            rightward(batch, piece, step).start()
        if step < lefts:
            leftward(batch, piece, step).start()

    steps = right_steps + 1
    waves = steps + pieces - 1

    def wave(batch, now):
        for piece in range(pieces):
            if 0 <= now - piece < steps:
                advance(batch, piece, now - piece)

    def waves_of_next(batch, low, high):
        if low < high:
            @pl.when(batch + 1 < batches)
            def _():
                for now in range(low, high):
                    wave(batch + 1, now)

    for now in range(waves):
        wave(0, now)

    spread = 8
    group = 128
    marks = [min(waves, mark) for mark in MARKS]

    def gather(start, stop):
        @pl.loop(start, stop)
        def _(chunk):
            base = pl.multiple_of(chunk * group, group)
            for lump in range(group // 16):
                picked = [xf[pl.ds(skel[base + lump * 16 + offset], 1), :] for offset in range(16)]
                xb[pl.ds(pl.multiple_of(base + lump * 16, 16), 16), :] = jnp.concatenate(picked, axis=0).astype(jnp.bfloat16)

    @pl.loop(0, batches)
    def _(batch):
        span = depth // spread
        waves_of_next(batch, 0, marks[0])

        @pl.loop(0, spread)
        def _(part):
            at = pl.ds(pl.multiple_of(part * span, span), span)
            xf[at, :] = recv[batch, at, :].astype(jnp.float32)

        chunks = depth // group
        for part in range(4):
            gather(part * chunks // 4, (part + 1) * chunks // 4)
            waves_of_next(batch, marks[part], marks[part + 1])

        for piece in range(pieces):
            @pl.when(batch == 0)
            def _():
                for part in range(2):
                    load(piece, part).wait()

            joined = jnp.dot(
                matrix[pl.ds(2 * piece * size, 2 * size), :], xb[...], preferred_element_type=jnp.float32
            )
            lane = lax.broadcasted_iota(jnp.int32, (size, width), 1)
            turned = pltpu.roll(joined[size:], half, axis=1)
            total = joined[:size] + jnp.where(lane < half, -turned, turned)
            at = pl.ds(piece * size, size)
            out[batch, at, :] = (total + src[batch, at, :].astype(jnp.float32)).astype(jnp.bfloat16)

            @pl.when(inner)
            def _():
                passing(batch, piece).start()

            low = marks[min(len(marks) - 1, piece + 4)]
            high = waves if piece == pieces - 1 else marks[min(len(marks) - 1, piece + 5)]
            waves_of_next(batch, low, high)

    @pl.loop(0, batches)
    def _(batch):
        for piece in range(pieces):
            rights, lefts = splits(piece)
            for step in range(rights):
                rightward(batch, piece, step).wait_send()
            for step in range(lefts):
                leftward(batch, piece, step).wait_send()

            @pl.when(inner)
            def _():
                passing(batch, piece).wait_send()


def on_device(rhs, operator, sources, skeleton):
    slabs = lax.axis_size("slab")
    count = lax.axis_size("row")
    batches, two, lanes, rows = rhs.shape
    depth = operator.shape[3]
    width = two * lanes
    flipped = rhs.reshape(batches, width, rows).transpose(0, 2, 1)
    added = sources[0].reshape(batches, width, rows).transpose(0, 2, 1)
    half = max(1, count // 2)
    pieces = 4 if count <= 8 else 1
    result = pl.pallas_call(
        functools.partial(kernel, slabs, count, pieces),
        out_shape=jax.ShapeDtypeStruct((batches, rows, width), jnp.bfloat16),
        in_specs=[
            pl.BlockSpec(memory_space=pltpu.SMEM),
            pl.BlockSpec(memory_space=pltpu.VMEM),
            pl.BlockSpec(memory_space=pl.ANY),
            pl.BlockSpec(memory_space=pltpu.VMEM),
        ],
        out_specs=pl.BlockSpec(memory_space=pltpu.VMEM),
        scratch_shapes=[
            pltpu.VMEM((2 * rows, depth), jnp.bfloat16),
            pltpu.VMEM((batches, depth, width), jnp.bfloat16),
            pltpu.VMEM((depth, width), jnp.float32),
            pltpu.VMEM((depth, width), jnp.bfloat16),
            pltpu.SemaphoreType.DMA((pieces, 2)),
            pltpu.SemaphoreType.DMA((batches,)),
            pltpu.SemaphoreType.DMA((batches, pieces, half)),
            pltpu.SemaphoreType.DMA((batches, pieces, half)),
            pltpu.SemaphoreType.DMA((batches, pieces, half)),
            pltpu.SemaphoreType.DMA((batches, pieces, half)),
            pltpu.SemaphoreType.DMA((batches, pieces)),
            pltpu.SemaphoreType.DMA((batches, pieces)),
        ],
        compiler_params=pltpu.CompilerParams(
            collective_id=0, has_side_effects=True, vmem_limit_bytes=60 * 1024 * 1024
        ),
    )(skeleton[0], flipped, operator[0], added)
    return result.transpose(0, 2, 1).reshape(batches, two, lanes, rows)[None]


def solution(mesh):
    return jax.shard_map(
        on_device,
        mesh=mesh,
        in_specs=(
            P(None, None, None, "row"),
            P("slab", None, "row", None),
            P("slab", None, None, None, "row"),
            P("slab", None),
        ),
        out_specs=P("slab", None, None, None, "row"),
        check_vma=False,
    )
```
